32 devices in a mesh: hst: 8 (over y, x, core), local: 4 (over z).
Axes of the slice: x: 2, y: 2, z: 4, core: 2. Of those that a mesh axis runs over, the one named last changes fastest.
Arguments:
- image_feats: bfloat16 [4096, 1152], P(('hst', 'local')), may hold values from -6 to 6
- text_feats: bfloat16 [4096, 1152], P(('hst', 'local')), may hold values from -6 to 6
- image_proj: bfloat16 [1152, 1152], replicated, may hold values from -0.1875 to 0.1875
- text_proj: bfloat16 [1152, 1152], replicated, may hold values from -0.1875 to 0.1875
- scale: float32 [1], replicated, may hold values from 4 to 16
- bias: float32 [1], replicated, may hold values from -4 to -2
Outputs:
- image_grad: float32 [4096, 1152], P(('hst', 'local'))
- text_grad: float32 [4096, 1152], P(('hst', 'local'))
The draws below stay inside these ranges and needn't reach their ends.
All inputs are finite; a program needn't handle non-finite values.
Results may differ from the reference program's by a relative error of at most 0.005.
Values may be sent and summed in bfloat16 or wider, within the bound.
A program may use at most 64 MiB of HBM per device.

```python
import math
import jax
import jax.numpy as jnp
from jax import lax

W = 1152
E = 1152
B_DEV = 128
GROUP_DEVS = 8
N = 4096


def steps_of(own_key, extent, shards, least, largest):
    level = 1.0
    for axis_at, parts in shards:
        steps = jax.random.uniform(jax.random.fold_in(jax.random.fold_in(own_key, 6), axis_at), (parts,), jnp.float32, least / len(shards), largest / len(shards))
        level = level * jnp.repeat(jnp.exp(steps), extent[axis_at] // parts).reshape((-1,) + (1,) * (len(extent) - 1 - axis_at))
    return level


def noise(stream_key, shape, scale, reach, split=(), kind=jnp.bfloat16):
    values = jax.random.normal(stream_key, shape, jnp.float32) * scale
    if len(split) > 0:
        values = steps_of(stream_key, shape, split, -0.22, 0.18) * values
    return jnp.clip(values, min=-reach, max=reach).astype(kind)


def setup_inputs(seed: int = 0) -> dict:
    key_of = jax.random.split(jax.random.key(seed), 7)
    image_feats = noise(key_of[0], (N, W), 1.0, 6.0, ((0, 32),))
    text_feats = noise(key_of[1], (N, W), 1.0, 6.0, ((0, 32),))
    image_proj = noise(key_of[2], (W, E), W ** -0.5, 0.1875)
    text_proj = noise(key_of[3], (W, E), W ** -0.5, 0.1875)
    scale = jnp.clip(jnp.exp(jax.random.uniform(key_of[4], (1,), jnp.float32, math.log(4.0), math.log(16.0))), 4.0, 16.0)
    bias = jnp.clip(jax.random.uniform(key_of[5], (1,), jnp.float32, -4.0, -2.0), -4.0, -2.0)
    return dict(image_feats=image_feats, text_feats=text_feats, image_proj=image_proj, text_proj=text_proj, scale=scale, bias=bias)


def project(feats, proj):
    raw_embed = jnp.dot(feats, proj, preferred_element_type=jnp.float32)
    recip = lax.rsqrt(lax.optimization_barrier(jnp.sum(raw_embed * raw_embed, axis=1, keepdims=True)) + 1e-06)
    unit = raw_embed * recip
    return (unit, recip, unit.astype(jnp.bfloat16))

def descend(unit, recip, grad_unit, proj):
    inner = lax.optimization_barrier(jnp.sum(unit * grad_unit, axis=1, keepdims=True))
    grad_raw = (recip * (grad_unit - unit * inner)).astype(jnp.bfloat16)
    return jnp.dot(grad_raw, proj.T, preferred_element_type=jnp.float32)

def reference(image_feats, text_feats, image_proj, text_proj, scale, bias):
    image_unit, image_recip, image_emb = project(image_feats, image_proj)
    text_unit, text_recip, text_emb = project(text_feats, text_proj)
    temper = scale[0]
    offset = bias[0]
    stride = N // (GROUP_DEVS * B_DEV)
    group_rows = GROUP_DEVS * B_DEV

    def regroup(values):
        return values.reshape(GROUP_DEVS, stride, B_DEV, E).transpose(1, 0, 2, 3).reshape(stride, group_rows, E)

    def ungroup(values):
        return values.reshape(stride, GROUP_DEVS, B_DEV, E).transpose(1, 0, 2, 3).reshape(N, E)
    matched = jnp.eye(group_rows, dtype=jnp.float32)

    def one_group(group_pair):
        image_rows, text_rows = group_pair
        logits = temper * jnp.dot(image_rows, text_rows.T, preferred_element_type=jnp.float32) + offset
        grad_logit = (jax.nn.sigmoid(logits) - matched).astype(jnp.bfloat16)
        image_part = jnp.dot(grad_logit, text_rows, preferred_element_type=jnp.float32)
        text_part = jnp.dot(grad_logit.T, image_rows, preferred_element_type=jnp.float32)
        return (image_part, text_part)
    image_parts, text_parts = lax.map(one_group, (regroup(image_emb), regroup(text_emb)))
    image_dz = temper * ungroup(image_parts)
    text_dz = temper * ungroup(text_parts)
    image_grad = descend(image_unit, image_recip, image_dz, image_proj)
    text_grad = descend(text_unit, text_recip, text_dz, text_proj)
    return (image_grad, text_grad)
```

```python
import functools

import jax
import jax.numpy as jnp
from jax import lax
from jax.experimental import pallas as pl
from jax.experimental.pallas import tpu as pltpu
from jax.sharding import PartitionSpec as P

GROUP_DEVS = 8
CHUNKS = 2
SIBLING, PARTNER, RELAY, BACK = range(4)


def flipped(member, bit):
    return member + bit - 2 * bit * lax.rem(lax.div(member, bit), 2)


def kernel(
    axis_sizes,
    image_feats,
    text_feats,
    image_proj,
    text_proj,
    scale,
    bias,
    image_grad,
    text_grad,
    feats,
    proj,
    emb,
    unit,
    recip,
    own_sum,
    away_sum,
    away_out,
    away_in,
    load_sem,
    send_sem,
    recv_sem,
):
    hosts, locals_ = axis_sizes
    stride = hosts * locals_ // GROUP_DEVS
    position = lax.axis_index("hst") * locals_ + lax.axis_index("local")
    member = lax.div(position, stride)
    rest = lax.rem(position, stride)

    def device_of(other):
        place = other * stride + rest
        return (lax.div(place, locals_), lax.rem(place, locals_))

    sibling = device_of(flipped(member, 1))
    partners = (device_of(flipped(member, 2)), device_of(flipped(member, 4)))

    rows = image_feats.shape[0]
    part = rows // CHUNKS
    temper = scale[0]
    offset = bias[0]

    feat_loads = []
    proj_loads = []
    for side, (feat_ref, proj_ref) in enumerate(
        ((image_feats, image_proj), (text_feats, text_proj))
    ):
        feat_loads.append(
            pltpu.make_async_copy(feat_ref, feats.at[side], load_sem.at[side, 0])
        )
        proj_loads.append(
            pltpu.make_async_copy(proj_ref, proj.at[side], load_sem.at[side, 1])
        )
        feat_loads[side].start()
        proj_loads[side].start()

    barrier = pltpu.get_barrier_semaphore()
    for other in (sibling,) + partners:
        pl.semaphore_signal(
            barrier, inc=1, device_id=other, device_id_type=pl.DeviceIdType.MESH
        )

    def remote(src, dst, kind, side, piece, device):
        return pltpu.make_async_remote_copy(
            src_ref=src,
            dst_ref=dst,
            send_sem=send_sem.at[kind, side, piece],
            recv_sem=recv_sem.at[kind, side, piece],
            device_id=device,
            device_id_type=pl.DeviceIdType.MESH,
        )

    copies = {}

    def send(kind, side, piece):
        span = pl.ds(piece * part, part)
        if kind == SIBLING:
            src, dst, device = emb.at[side, 0, span], emb.at[side, 1, span], sibling
        elif kind == PARTNER:
            src, dst, device = emb.at[side, 0, span], emb.at[side, 2, span], partners[side]
        elif kind == RELAY:
            src, dst, device = emb.at[side, 2, span], emb.at[side, 3, span], sibling
        else:
            src, dst, device = away_out.at[side, span], away_in.at[side, span], partners[side]
        copy = remote(src, dst, kind, side, piece, device)
        copy.start()
        copies[kind, side, piece] = copy

    for side in range(2):
        feat_loads[side].wait()
        proj_loads[side].wait()
        raw = jnp.dot(feats[side], proj[side], preferred_element_type=jnp.float32)
        inverse = lax.rsqrt(jnp.sum(raw * raw, axis=1, keepdims=True) + 1e-06)
        normal = raw * inverse
        unit[side] = normal
        recip[side] = inverse
        emb[side, 0] = normal.astype(jnp.bfloat16)
        if side == 0:
            pl.semaphore_wait(barrier, 3)
        for piece in range(CHUNKS):
            send(PARTNER, side, piece)
        for piece in range(CHUNKS):
            send(SIBLING, side, piece)

    def pull(side, row_slot, first, last):
        mine = emb[side, row_slot]
        theirs = emb[1 - side, first:last].reshape((last - first) * rows, mine.shape[1])
        logits = temper * lax.dot_general(
            mine, theirs, (((1,), (1,)), ((), ())), preferred_element_type=jnp.float32
        ) + offset
        slope = jax.nn.sigmoid(logits)
        if row_slot == 0 and first == 0:
            down = lax.broadcasted_iota(jnp.int32, slope.shape, 0)
            along = lax.broadcasted_iota(jnp.int32, slope.shape, 1)
            slope = slope - jnp.where(down == along, 1.0, 0.0)
        return jnp.dot(
            slope.astype(jnp.bfloat16), theirs, preferred_element_type=jnp.float32
        )

    for side in range(2):
        for piece in range(CHUNKS):
            copies[SIBLING, side, piece].wait_recv()
    for side in range(2):
        own_sum[side] = pull(side, 0, 0, 2)

    for piece in range(CHUNKS):
        for side in range(2):
            copies[PARTNER, side, piece].wait_recv()
            send(RELAY, side, piece)
    for side in (1, 0):
        away_sum[side] = pull(side, 2, 0, 3)

    for side in (1, 0):
        for piece in range(CHUNKS):
            copies[RELAY, 1 - side, piece].wait_recv()
        away_out[side] = (away_sum[side] + pull(side, 2, 3, 4)).astype(jnp.bfloat16)
        for piece in range(CHUNKS):
            send(BACK, side, piece)
    for side in (1, 0):
        own_sum[side] += pull(side, 0, 2, 4)

    outs = (image_grad, text_grad)
    for piece in range(CHUNKS):
        span = pl.ds(piece * part, part)
        for side in (1, 0):
            copies[BACK, side, piece].wait_recv()
            slope = temper * (own_sum[side, span] + away_in[side, span].astype(jnp.float32))
            normal = unit[side, span]
            inner = jnp.sum(normal * slope, axis=1, keepdims=True)
            down = (recip[side, span] * (slope - normal * inner)).astype(jnp.bfloat16)
            outs[side][span] = lax.dot_general(
                down, proj[side], (((1,), (1,)), ((), ())), preferred_element_type=jnp.float32
            )

    for copy in copies.values():
        copy.wait_send()


def on_device(axis_sizes, image_feats, text_feats, image_proj, text_proj, scale, bias):
    rows, width = image_feats.shape
    embed = image_proj.shape[1]
    out = jax.ShapeDtypeStruct((rows, width), jnp.float32)
    anywhere = pl.BlockSpec(memory_space=pl.ANY)
    scalar = pl.BlockSpec(memory_space=pltpu.SMEM)
    vmem = pl.BlockSpec(memory_space=pltpu.VMEM)
    return pl.pallas_call(
        functools.partial(kernel, axis_sizes),
        out_shape=(out, out),
        in_specs=[anywhere] * 4 + [scalar] * 2,
        out_specs=(vmem, vmem),
        scratch_shapes=[
            pltpu.VMEM((2, rows, width), jnp.bfloat16),
            pltpu.VMEM((2, width, embed), jnp.bfloat16),
            pltpu.VMEM((2, 4, rows, embed), jnp.bfloat16),
            pltpu.VMEM((2, rows, embed), jnp.float32),
            pltpu.VMEM((2, rows, 1), jnp.float32),
            pltpu.VMEM((2, rows, embed), jnp.float32),
            pltpu.VMEM((2, rows, embed), jnp.float32),
            pltpu.VMEM((2, rows, embed), jnp.bfloat16),
            pltpu.VMEM((2, rows, embed), jnp.bfloat16),
            pltpu.SemaphoreType.DMA((2, 2)),
            pltpu.SemaphoreType.DMA((4, 2, CHUNKS)),
            pltpu.SemaphoreType.DMA((4, 2, CHUNKS)),
        ],
        compiler_params=pltpu.CompilerParams(
            collective_id=0, has_side_effects=True, vmem_limit_bytes=48 * 1024 * 1024
        ),
    )(image_feats, text_feats, image_proj, text_proj, scale, bias)


def solution(mesh):
    in_specs = (P(("hst", "local"), None), P(("hst", "local"), None), P(), P(), P(), P())
    out_specs = (P(("hst", "local"), None), P(("hst", "local"), None))
    axis_sizes = (mesh.shape["hst"], mesh.shape["local"])
    return jax.shard_map(
        functools.partial(on_device, axis_sizes),
        mesh=mesh,
        in_specs=in_specs,
        out_specs=out_specs,
        check_vma=False,
    )
```

```python
import functools

import jax
import jax.numpy as jnp
from jax import lax
from jax.experimental import pallas as pl
from jax.experimental.pallas import tpu as pltpu
from jax.sharding import PartitionSpec as P

GROUP_DEVS = 8
CHUNKS = 2
BACK_CHUNKS = 2
SIBLING, PARTNER, RELAY, BACK = range(4)


def flipped(member, bit):
    return member + bit - 2 * bit * lax.rem(lax.div(member, bit), 2)


def kernel(
    axis_sizes,
    image_feats,
    text_feats,
    image_proj,
    text_proj,
    knobs,
    image_grad,
    text_grad,
    feats,
    away_feats,
    proj,
    proj_t,
    emb,
    unit,
    recip,
    own_sum,
    away_sum,
    away_out,
    away_in,
    load_sem,
    send_sem,
    recv_sem,
):
    hosts, locals_ = axis_sizes
    stride = hosts * locals_ // GROUP_DEVS
    position = lax.axis_index("hst") * locals_ + lax.axis_index("local")
    member = lax.div(position, stride)
    rest = lax.rem(position, stride)

    def device_of(other):
        place = other * stride + rest
        return (lax.div(place, locals_), lax.rem(place, locals_))

    sibling = device_of(flipped(member, 1))
    partners = (device_of(flipped(member, 2)), device_of(flipped(member, 4)))

    rows = image_feats.shape[0]
    part = rows // CHUNKS
    feat_loads = []
    proj_loads = []
    for side, (feat_ref, proj_ref) in enumerate(
        ((image_feats, image_proj), (text_feats, text_proj))
    ):
        feat_loads.append(
            pltpu.make_async_copy(feat_ref, feats.at[side], load_sem.at[side, 0])
        )
        proj_loads.append(
            pltpu.make_async_copy(proj_ref, proj.at[side], load_sem.at[side, 1])
        )
        feat_loads[side].start()
        proj_loads[side].start()

    barrier = pltpu.get_barrier_semaphore()
    for other in (sibling,) + partners:
        pl.semaphore_signal(
            barrier, inc=1, device_id=other, device_id_type=pl.DeviceIdType.MESH
        )

    def remote(src, dst, kind, side, piece, device):
        return pltpu.make_async_remote_copy(
            src_ref=src,
            dst_ref=dst,
            send_sem=send_sem.at[kind, side, piece],
            recv_sem=recv_sem.at[kind, side, piece],
            device_id=device,
            device_id_type=pl.DeviceIdType.MESH,
        )

    copies = {}
    given = (image_feats, text_feats)

    def send(kind, side, piece):
        size = rows // (BACK_CHUNKS if kind == BACK else CHUNKS)
        span = pl.ds(piece * size, size)
        if kind == SIBLING:
            src, dst, device = emb.at[side, 0, span], emb.at[side, 1, span], sibling
        elif kind == PARTNER:
            src, dst, device = given[side].at[span], away_feats.at[side, span], partners[side]
        elif kind == RELAY:
            src, dst, device = emb.at[side, 2, span], emb.at[side, 3, span], sibling
        else:
            src, dst, device = away_out.at[side, span], away_in.at[side, span], partners[side]
        copy = remote(src, dst, kind, side, piece, device)
        copy.start()
        copies[kind, side, piece] = copy

    pl.semaphore_wait(barrier, 3)
    for piece in range(CHUNKS):
        for side in range(2):
            send(PARTNER, side, piece)

    def embed(rows_in, side):
        raw = jnp.dot(rows_in, proj[side], preferred_element_type=jnp.float32)
        inverse = lax.rsqrt(jnp.sum(raw * raw, axis=1, keepdims=True) + 1e-06)
        return raw * inverse, inverse

    for side in range(2):
        feat_loads[side].wait()
        proj_loads[side].wait()
        normal, inverse = embed(feats[side], side)
        unit[side] = normal
        recip[side] = inverse
        emb[side, 0] = normal.astype(jnp.bfloat16)
        for piece in range(CHUNKS):
            send(SIBLING, side, piece)

    temper = knobs[0:1, 0:1]
    offset = knobs[1:2, 0:1]

    def pull(side, row_slot, span, first, last):
        mine = emb[side, row_slot, span]
        theirs = emb[1 - side, first:last].reshape((last - first) * rows, mine.shape[1])
        logits = temper * lax.dot_general(
            mine, theirs, (((1,), (1,)), ((), ())), preferred_element_type=jnp.float32
        ) + offset
        slope = jax.nn.sigmoid(logits)
        if row_slot == 0 and first == 0:
            down = lax.broadcasted_iota(jnp.int32, slope.shape, 0)
            along = lax.broadcasted_iota(jnp.int32, slope.shape, 1)
            slope = slope - jnp.where(down == along, 1.0, 0.0)
        return jnp.dot(
            slope.astype(jnp.bfloat16), theirs, preferred_element_type=jnp.float32
        )

    whole = pl.ds(0, rows)
    for side in range(2):
        for piece in range(CHUNKS):
            copies[SIBLING, side, piece].wait_recv()
    for side in range(2):
        own_sum[side] = pull(side, 0, whole, 0, 2)

    for piece in range(CHUNKS):
        span = pl.ds(piece * part, part)
        for side in range(2):
            copies[PARTNER, side, piece].wait_recv()
            emb[side, 2, span] = embed(away_feats[side, span], side)[0].astype(jnp.bfloat16)
            send(RELAY, side, piece)
        for side in (1, 0):
            away_sum[side, span] = pull(side, 2, span, 0, 2)
        if piece == 0:
            for side in range(2):
                proj_t[side] = proj[side].T
    for side in (1, 0):
        away_sum[side] += pull(side, 2, whole, 2, 3)

    for side in (1, 0):
        for piece in range(CHUNKS):
            copies[RELAY, 1 - side, piece].wait_recv()
        away_out[side] = (away_sum[side] + pull(side, 2, whole, 3, 4)).astype(jnp.bfloat16)
        for piece in range(BACK_CHUNKS):
            send(BACK, side, piece)
    for side in (1, 0):
        own_sum[side] += pull(side, 0, whole, 2, 4)

    outs = (image_grad, text_grad)
    part = rows // BACK_CHUNKS
    for piece in range(BACK_CHUNKS):
        span = pl.ds(piece * part, part)
        for side in (1, 0):
            copies[BACK, side, piece].wait_recv()
            slope = temper * (own_sum[side, span] + away_in[side, span].astype(jnp.float32))
            normal = unit[side, span]
            inner = jnp.sum(normal * slope, axis=1, keepdims=True)
            down = (recip[side, span] * (slope - normal * inner)).astype(jnp.bfloat16)
            outs[side][span] = jnp.dot(
                down, proj_t[side], preferred_element_type=jnp.float32
            )

    for copy in copies.values():
        copy.wait_send()


def on_device(axis_sizes, image_feats, text_feats, image_proj, text_proj, scale, bias):
    rows, width = image_feats.shape
    embed = image_proj.shape[1]
    out = jax.ShapeDtypeStruct((rows, width), jnp.float32)
    anywhere = pl.BlockSpec(memory_space=pltpu.HBM)
    vmem = pl.BlockSpec(memory_space=pltpu.VMEM)
    return pl.pallas_call(
        functools.partial(kernel, axis_sizes),
        out_shape=(out, out),
        in_specs=[anywhere] * 4 + [vmem],
        out_specs=(vmem, vmem),
        scratch_shapes=[
            pltpu.VMEM((2, rows, width), jnp.bfloat16),
            pltpu.VMEM((2, rows, width), jnp.bfloat16),
            pltpu.VMEM((2, width, embed), jnp.bfloat16),
            pltpu.VMEM((2, embed, width), jnp.bfloat16),
            pltpu.VMEM((2, 4, rows, embed), jnp.bfloat16),
            pltpu.VMEM((2, rows, embed), jnp.float32),
            pltpu.VMEM((2, rows, 1), jnp.float32),
            pltpu.VMEM((2, rows, embed), jnp.float32),
            pltpu.VMEM((2, rows, embed), jnp.float32),
            pltpu.VMEM((2, rows, embed), jnp.bfloat16),
            pltpu.VMEM((2, rows, embed), jnp.bfloat16),
            pltpu.SemaphoreType.DMA((2, 2)),
            pltpu.SemaphoreType.DMA((4, 2, max(CHUNKS, BACK_CHUNKS))),
            pltpu.SemaphoreType.DMA((4, 2, max(CHUNKS, BACK_CHUNKS))),
        ],
        compiler_params=pltpu.CompilerParams(
            collective_id=0, has_side_effects=True, vmem_limit_bytes=52428800
        ),
    )(
        *(pltpu.with_memory_space_constraint(x, pltpu.HBM) for x in (image_feats, text_feats, image_proj, text_proj)), jnp.broadcast_to(jnp.stack([scale, bias]), (2, 128))
    )


def solution(mesh):
    in_specs = (P(("hst", "local"), None), P(("hst", "local"), None), P(), P(), P(), P())
    out_specs = (P(("hst", "local"), None), P(("hst", "local"), None))
    axis_sizes = (mesh.shape["hst"], mesh.shape["local"])
    return jax.shard_map(
        functools.partial(on_device, axis_sizes),
        mesh=mesh,
        in_specs=in_specs,
        out_specs=out_specs,
        check_vma=False,
    )
```

```python
import functools

import jax
import jax.numpy as jnp
from jax import lax
from jax.experimental import pallas as pl
from jax.experimental.pallas import tpu as pltpu
from jax.sharding import PartitionSpec as P

GROUP_DEVS = 8
CHUNKS = 2
BACK_CHUNKS = 2
SIBLING, PARTNER, RELAY, BACK = range(4)


def flipped(member, bit):
    return member + bit - 2 * bit * lax.rem(lax.div(member, bit), 2)


def kernel(
    axis_sizes,
    image_feats,
    text_feats,
    image_proj,
    text_proj,
    knobs,
    image_grad,
    text_grad,
    feats,
    away_feats,
    proj,
    proj_t,
    emb,
    unit,
    recip,
    own_sum,
    away_sum,
    away_out,
    away_in,
    load_sem,
    send_sem,
    recv_sem,
):
    hosts, locals_ = axis_sizes
    stride = hosts * locals_ // GROUP_DEVS
    position = lax.axis_index("hst") * locals_ + lax.axis_index("local")
    member = lax.div(position, stride)
    rest = lax.rem(position, stride)

    def device_of(other):
        place = other * stride + rest
        return (lax.div(place, locals_), lax.rem(place, locals_))

    sibling = device_of(flipped(member, 1))
    partners = (device_of(flipped(member, 2)), device_of(flipped(member, 4)))

    rows = image_feats.shape[0]
    part = rows // CHUNKS
    feat_loads = []
    proj_loads = []
    for side, (feat_ref, proj_ref) in enumerate(
        ((image_feats, image_proj), (text_feats, text_proj))
    ):
        feat_loads.append(
            pltpu.make_async_copy(feat_ref, feats.at[side], load_sem.at[side, 0])
        )
        proj_loads.append(
            pltpu.make_async_copy(proj_ref, proj.at[side], load_sem.at[side, 1])
        )
        feat_loads[side].start()
        proj_loads[side].start()

    barrier = pltpu.get_barrier_semaphore()
    for other in (sibling,) + partners:
        pl.semaphore_signal(
            barrier, inc=1, device_id=other, device_id_type=pl.DeviceIdType.MESH
        )

    def remote(src, dst, kind, side, piece, device):
        return pltpu.make_async_remote_copy(
            src_ref=src,
            dst_ref=dst,
            send_sem=send_sem.at[kind, side, piece],
            recv_sem=recv_sem.at[kind, side, piece],
            device_id=device,
            device_id_type=pl.DeviceIdType.MESH,
        )

    copies = {}
    given = (image_feats, text_feats)

    def send(kind, side, piece):
        size = rows // (BACK_CHUNKS if kind == BACK else CHUNKS)
        span = pl.ds(piece * size, size)
        if kind == SIBLING:
            src, dst, device = emb.at[side, 0, span], emb.at[side, 1, span], sibling
        elif kind == PARTNER:
            src, dst, device = given[side].at[span], away_feats.at[side, span], partners[side]
        elif kind == RELAY:
            src, dst, device = emb.at[side, 2, span], emb.at[side, 3, span], sibling
        else:
            src, dst, device = away_out.at[side, span], away_in.at[side, span], partners[side]
        copy = remote(src, dst, kind, side, piece, device)
        copy.start()
        copies[kind, side, piece] = copy

    pl.semaphore_wait(barrier, 3)
    for piece in range(CHUNKS):
        for side in range(2):
            send(PARTNER, side, piece)

    def embed(rows_in, side):
        raw = jnp.dot(rows_in, proj[side], preferred_element_type=jnp.float32)
        inverse = lax.rsqrt(jnp.sum(raw * raw, axis=1, keepdims=True) + 1e-06)
        return raw * inverse, inverse

    for side in range(2):
        feat_loads[side].wait()
        proj_loads[side].wait()
        normal, inverse = embed(feats[side], side)
        unit[side] = normal
        recip[side] = inverse
        emb[side, 0] = normal.astype(jnp.bfloat16)
        for piece in range(CHUNKS):
            send(SIBLING, side, piece)

    temper = knobs[0:1, 0:1]
    offset = knobs[1:2, 0:1]

    def pull(side, row_slot, span, first, last):
        mine = emb[side, row_slot, span]
        theirs = emb[1 - side, first:last].reshape((last - first) * rows, mine.shape[1])
        logits = temper * lax.dot_general(
            mine, theirs, (((1,), (1,)), ((), ())), preferred_element_type=jnp.float32
        ) + offset
        slope = jax.nn.sigmoid(logits)
        if row_slot == 0 and first == 0:
            down = lax.broadcasted_iota(jnp.int32, slope.shape, 0)
            along = lax.broadcasted_iota(jnp.int32, slope.shape, 1)
            slope = slope - jnp.where(down == along, 1.0, 0.0)
        return jnp.dot(
            slope.astype(jnp.bfloat16), theirs, preferred_element_type=jnp.float32
        )

    whole = pl.ds(0, rows)
    for side in range(2):
        for piece in range(CHUNKS):
            copies[SIBLING, side, piece].wait_recv()
    for side in range(2):
        own_sum[side] = pull(side, 0, whole, 0, 2)

    for piece in range(CHUNKS):
        span = pl.ds(piece * part, part)
        for side in range(2):
            copies[PARTNER, side, piece].wait_recv()
            emb[side, 2, span] = embed(away_feats[side, span], side)[0].astype(jnp.bfloat16)
            send(RELAY, side, piece)
        for side in (1, 0):
            away_sum[side, span] = pull(side, 2, span, 0, 2)
    for side in (1, 0):
        away_sum[side] += pull(side, 2, whole, 2, 3)

    for side in (1, 0):
        for piece in range(CHUNKS):
            copies[RELAY, 1 - side, piece].wait_recv()
        away_out[side] = (away_sum[side] + pull(side, 2, whole, 3, 4)).astype(jnp.bfloat16)
        for piece in range(BACK_CHUNKS):
            send(BACK, side, piece)
    for side in (1, 0):
        own_sum[side] += pull(side, 0, whole, 2, 4)
    for side in (1, 0):
        proj_t[side] = proj[side].T

    outs = (image_grad, text_grad)
    part = rows // BACK_CHUNKS
    for piece in range(BACK_CHUNKS):
        span = pl.ds(piece * part, part)
        for side in (1, 0):
            copies[BACK, side, piece].wait_recv()
            slope = temper * (own_sum[side, span] + away_in[side, span].astype(jnp.float32))
            normal = unit[side, span]
            inner = jnp.sum(normal * slope, axis=1, keepdims=True)
            down = (recip[side, span] * (slope - normal * inner)).astype(jnp.bfloat16)
            outs[side][span] = jnp.dot(
                down, proj_t[side], preferred_element_type=jnp.float32
            )

    for copy in copies.values():
        copy.wait_send()


def on_device(axis_sizes, image_feats, text_feats, image_proj, text_proj, scale, bias):
    rows, width = image_feats.shape
    embed = image_proj.shape[1]
    out = jax.ShapeDtypeStruct((rows, width), jnp.float32)
    anywhere = pl.BlockSpec(memory_space=pltpu.HBM)
    vmem = pl.BlockSpec(memory_space=pltpu.VMEM)
    return pl.pallas_call(
        functools.partial(kernel, axis_sizes),
        out_shape=(out, out),
        in_specs=[anywhere] * 4 + [vmem],
        out_specs=(vmem, vmem),
        scratch_shapes=[
            pltpu.VMEM((2, rows, width), jnp.bfloat16),
            pltpu.VMEM((2, rows, width), jnp.bfloat16),
            pltpu.VMEM((2, width, embed), jnp.bfloat16),
            pltpu.VMEM((2, embed, width), jnp.bfloat16),
            pltpu.VMEM((2, 4, rows, embed), jnp.bfloat16),
            pltpu.VMEM((2, rows, embed), jnp.float32),
            pltpu.VMEM((2, rows, 1), jnp.float32),
            pltpu.VMEM((2, rows, embed), jnp.float32),
            pltpu.VMEM((2, rows, embed), jnp.float32),
            pltpu.VMEM((2, rows, embed), jnp.bfloat16),
            pltpu.VMEM((2, rows, embed), jnp.bfloat16),
            pltpu.SemaphoreType.DMA((2, 2)),
            pltpu.SemaphoreType.DMA((4, 2, max(CHUNKS, BACK_CHUNKS))),
            pltpu.SemaphoreType.DMA((4, 2, max(CHUNKS, BACK_CHUNKS))),
        ],
        compiler_params=pltpu.CompilerParams(
            collective_id=0, has_side_effects=True, vmem_limit_bytes=52428800
        ),
    )(
        *(pltpu.with_memory_space_constraint(x, pltpu.HBM) for x in (image_feats, text_feats, image_proj, text_proj)), jnp.broadcast_to(jnp.stack([scale, bias]), (2, 128))
    )


def solution(mesh):
    in_specs = (P(("hst", "local"), None), P(("hst", "local"), None), P(), P(), P(), P())
    out_specs = (P(("hst", "local"), None), P(("hst", "local"), None))
    axis_sizes = (mesh.shape["hst"], mesh.shape["local"])
    return jax.shard_map(
        functools.partial(on_device, axis_sizes),
        mesh=mesh,
        in_specs=in_specs,
        out_specs=out_specs,
        check_vma=False,
    )
```
